32 devices in a mesh: groups: 2 (over y), streams: 8 (over z, x), segment: 2 (over core).
Axes of the slice: x: 2, y: 2, z: 4, core: 2. Of those that a mesh axis runs over, the one named last changes fastest.
Arguments:
- latent: bfloat16 [4096, 1024], P(('groups', 'streams'), 'segment'), parts along dimension 0, may hold values from -6 to 6
- conv_weight: bfloat16 [1024, 16, 512], P('streams', None, 'segment'), may hold values from -0.1875 to 0.1875
- conv_bias: float32 [512], P('segment'), may hold values from -3 to 3
- tail_cache: bfloat16 [128, 8, 512], P(('groups', 'streams'), None, 'segment'), parts along dimension 0, may hold values from -6 to 6
- input_cache: bfloat16 [128, 2, 512], P(('groups', 'streams'), None, 'segment'), parts along dimension 0, may hold values from -0.8984375 to 2
- resume_slot: int32 [128], P(('groups', 'streams')), parts along dimension 0, may hold values from -1 to 255, as said below
- res_weight: bfloat16 [3, 512, 256], P(None, 'segment'), may hold values from -0.15625 to 0.15625
- res_bias: float32 [256], replicated, may hold values from -3 to 3
- skip_weight: bfloat16 [256, 512], P(None, 'segment'), may hold values from -0.375 to 0.375
- skip_bias: float32 [512], P('segment'), may hold values from -3 to 3
Outputs:
- decoded: bfloat16 [4096, 8, 512], P(('groups', 'streams'), None, 'segment'), parts along dimension 0
- new_tail: bfloat16 [4096, 8, 512], P(('groups', 'streams'), None, 'segment'), parts along dimension 0
The draws below stay inside these ranges and needn't reach their ends.
There are 2 independent parts, one for each index of `groups`. The reference program is written for one: setup_inputs(seed, part) draws one part's arguments, and reference() takes and returns one part's arrays. A program takes and returns all parts, laid end to end along the dimension named above; an argument that names none is the same for every part. Nothing has to cross between parts.
Inputs may be any that keep to these rules, and one draw needn't show every extreme that they name: `resume_slot`: slot k of an owner device's store serves decoder device k // 1 of the same index range; an entry is -1 (slot unused) or the position, among that decoder device's 256 rows in decoder order, of the session that resumes from it. No decoder row is named by two slots. In every draw there is one decoder device all of whose reserved slots are in use (none is -1).
All inputs are finite; a program needn't handle non-finite values.
Results may differ from the reference program's by a relative error of at most 0.0042.
Values may be sent and summed in bfloat16 or wider, within the bound.
A program may use at most 64 MiB of HBM per device.

```python
import jax
import jax.numpy as jnp
from jax import lax

D = 1024
C1 = 512
HID = 256
STRIDE = 8
RES_K = 3
CAP = 1
S_DEV = 256
KERNEL = 16
SESSIONS = 2048
SLOTS = 64
N_STREAMS = 8


def draw_resume_slot(key, part):
    incoming_count = N_STREAMS * CAP
    device_keys = jax.random.split(jax.random.fold_in(key, 11), N_STREAMS)
    orders = jax.vmap(lambda single: jax.random.permutation(single, S_DEV))(device_keys)
    incoming = orders[:, :incoming_count].astype(jnp.int32)
    full_device = jax.random.randint(jax.random.fold_in(key, 12), (), 0, N_STREAMS)
    device_ids = jnp.arange(N_STREAMS, dtype=jnp.int32)[:, None]
    offsets = jnp.where(device_ids == full_device, S_DEV - 1 - incoming[:, :1], 0)
    incoming = (incoming + offsets) % S_DEV
    coins = jax.random.randint(jax.random.fold_in(key, 13), (N_STREAMS, incoming_count), 0, 2)
    used = (coins == 1) | (device_ids == full_device)
    named = jnp.where(used, incoming, -1)
    named = named.reshape(N_STREAMS, N_STREAMS, CAP).transpose(1, 0, 2)
    return named.reshape(-1).astype(jnp.int32)


def levels(rng, dims, cuts, low, top_value):
    loudness, own = 1.0, jax.random.fold_in(rng, 6)
    for position, blocks in cuts:
        heights = jnp.exp(jax.random.uniform(jax.random.fold_in(own, position), (blocks,), jnp.float32, low / len(cuts), top_value / len(cuts)))
        loudness = loudness * jnp.repeat(heights, dims[position] // blocks).reshape([-1 if axis == position else 1 for axis in range(len(dims))])
    return loudness


def noise(key, shape, scale, bound, cuts=(), held_as=jnp.bfloat16):
    drawn = scale * jax.random.normal(key, shape, jnp.float32)
    if cuts:
        drawn = drawn * levels(key, shape, cuts, -0.22, 0.18)
    return jnp.clip(drawn, -bound, bound).astype(held_as)


def setup_inputs(seed: int = 0, part: int = 0) -> dict:
    streams_of = jax.random.split(jax.random.key(seed), 11)
    part_splits = jax.random.split(jax.random.fold_in(streams_of[10], part), 11)
    latent = noise(part_splits[0], (SESSIONS, D), 1.0, 6.0, ((0, 8), (1, 2)))
    conv_weight = noise(streams_of[1], (D, KERNEL, C1), D ** -0.5, 0.1875, ((0, 8), (2, 2)))
    conv_bias = noise(streams_of[2], (C1,), 0.5, 3.0, ((0, 2),), jnp.float32)
    tail_cache = noise(part_splits[3], (SLOTS, STRIDE, C1), 1.0, 6.0, ((0, 8), (2, 2)))
    input_cache = jnp.clip(-0.8984375 + 2.8984375 * jax.random.uniform(part_splits[4], (SLOTS, RES_K - 1, C1), jnp.float32) ** levels(part_splits[4], (SLOTS, RES_K - 1, C1), ((0, 8), (2, 2)), -0.2, 0.2), -0.8984375, 2.0).astype(jnp.bfloat16)
    resume_slot = draw_resume_slot(jax.random.fold_in(jax.random.fold_in(streams_of[10], part), 71), part)
    res_weight = noise(streams_of[6], (RES_K, C1, HID), (RES_K * C1) ** -0.5, 0.15625, ((1, 2),))
    res_bias = noise(streams_of[7], (HID,), 0.5, 3.0, (), jnp.float32)
    skip_weight = noise(streams_of[8], (HID, C1), HID ** -0.5, 0.375, ((1, 2),))
    skip_bias = noise(streams_of[9], (C1,), 0.5, 3.0, ((0, 2),), jnp.float32)
    return dict(latent=latent, conv_weight=conv_weight, conv_bias=conv_bias, tail_cache=tail_cache, input_cache=input_cache, resume_slot=resume_slot, res_weight=res_weight, res_bias=res_bias, skip_weight=skip_weight, skip_bias=skip_bias)


def apply_elu(values):
    return jnp.where(values > 0, values, jnp.expm1(jnp.minimum(values, 0.0)))


def reference(latent, conv_weight, conv_bias, tail_cache, input_cache, resume_slot, res_weight, res_bias, skip_weight, skip_bias):
    lanes = N_STREAMS
    portion = S_DEV // lanes
    ordered = latent.reshape(lanes, lanes, portion, D).transpose(1, 0, 2, 3).reshape(lanes, S_DEV, D)
    tails = tail_cache.reshape(lanes, lanes, CAP, STRIDE * C1).transpose(1, 0, 2, 3).reshape(lanes, lanes * CAP, STRIDE * C1)
    inputs = input_cache.reshape(lanes, lanes, CAP, (RES_K - 1) * C1).transpose(1, 0, 2, 3).reshape(lanes, lanes * CAP, (RES_K - 1) * C1)
    slots = resume_slot.reshape(lanes, lanes, CAP).transpose(1, 0, 2).reshape(lanes, lanes * CAP)
    kernel_flat = conv_weight.reshape(D, KERNEL * C1)
    positions = jnp.arange(S_DEV, dtype=jnp.int32)

    def one_block(block):
        rows_in, tail_rows, input_rows, slot_rows = block
        excitation = apply_elu(rows_in.astype(jnp.float32)).astype(jnp.bfloat16)
        spread = jnp.dot(excitation, kernel_flat, preferred_element_type=jnp.float32).reshape(S_DEV, KERNEL, C1)
        one_hot = (slot_rows[None, :] == positions[:, None]).astype(jnp.bfloat16)
        prev_tail = jnp.dot(one_hot, tail_rows, preferred_element_type=jnp.float32).reshape(S_DEV, STRIDE, C1)
        prev_input = jnp.dot(one_hot, input_rows, preferred_element_type=jnp.float32).reshape(S_DEV, RES_K - 1, C1)
        upsampled = spread[:, :STRIDE] + prev_tail + conv_bias
        carried = spread[:, STRIDE:].astype(jnp.bfloat16)
        excited = apply_elu(upsampled).astype(jnp.bfloat16)
        window = jnp.concatenate([prev_input.astype(jnp.bfloat16), excited], axis=1).astype(jnp.float32)
        branch = jnp.zeros((S_DEV, STRIDE, HID), jnp.float32) + res_bias
        for offset in range(RES_K):
            branch = branch + jnp.einsum("stc,ch->sth", window[:, offset:offset + STRIDE], res_weight[offset].astype(jnp.float32))
        hidden = apply_elu(branch).astype(jnp.bfloat16)
        mixed = upsampled + jnp.einsum("sth,hc->stc", hidden.astype(jnp.float32), skip_weight.astype(jnp.float32)) + skip_bias
        return mixed.astype(jnp.bfloat16), carried

    decoded, new_tail = lax.map(one_block, (ordered, tails, inputs, slots))
    return decoded.reshape(lanes * S_DEV, STRIDE, C1), new_tail.reshape(lanes * S_DEV, STRIDE, C1)
```

```python
import jax
import jax.numpy as jnp
from jax import lax
from jax.experimental import pallas as pl
from jax.experimental.pallas import tpu as pltpu
from jax.sharding import PartitionSpec as P


def apply_elu(values):
    return jnp.where(values > 0, values, jnp.expm1(jnp.minimum(values, 0.0)))


def local(
    latent,
    conv_weight,
    conv_bias,
    tail_cache,
    input_cache,
    resume_slot,
    res_weight,
    res_bias,
    skip_weight,
    skip_bias,
):
    handed = lax.all_to_all(latent, "streams", split_axis=0, concat_axis=0, tiled=True)
    excitation_half = apply_elu(handed.astype(jnp.float32)).astype(jnp.bfloat16)
    excitation = lax.all_gather(excitation_half, "segment", axis=1, tiled=True)
    session_rows = excitation.shape[0]
    tap_count = conv_weight.shape[1]
    half_taps = tap_count // 2
    half_width = conv_weight.shape[2]
    piece = lax.all_gather(conv_weight, "streams", axis=0, tiled=True)
    kernel_rows = piece.reshape(piece.shape[0], tap_count * half_width)
    spread = jnp.dot(excitation, kernel_rows, preferred_element_type=jnp.float32)
    spread = spread.reshape(session_rows, tap_count, half_width)
    fetched_tail, fetched_input, fetched_slot = (
        lax.all_to_all(tail_cache, "streams", split_axis=0, concat_axis=0, tiled=True),
        lax.all_to_all(input_cache, "streams", split_axis=0, concat_axis=0, tiled=True),
        lax.all_to_all(resume_slot, "streams", split_axis=0, concat_axis=0, tiled=True),
    )
    arrivals = fetched_slot.shape[0]
    state_steps = fetched_input.shape[1]
    packed = jnp.concatenate(
        [fetched_tail.reshape(arrivals, -1), fetched_input.reshape(arrivals, -1)], axis=1
    )
    one_hot = (fetched_slot[None, :] == jnp.arange(session_rows, dtype=jnp.int32)[:, None]).astype(
        jnp.bfloat16
    )
    placed = jnp.dot(one_hot, packed, preferred_element_type=jnp.float32)
    prev_tail = placed[:, : half_taps * half_width].reshape(session_rows, half_taps, half_width)
    prev_input = (
        placed[:, half_taps * half_width :]
        .reshape(session_rows, state_steps, half_width)
        .astype(jnp.bfloat16)
    )
    upsampled = spread[:, :half_taps] + prev_tail + conv_bias
    new_tail = spread[:, half_taps:].astype(jnp.bfloat16)
    excited = apply_elu(upsampled).astype(jnp.bfloat16)
    window = jnp.concatenate([prev_input, excited], axis=1)
    hidden_width = res_weight.shape[2]
    partial_value = jnp.zeros((session_rows * half_taps, hidden_width), jnp.float32)
    for offset in range(res_weight.shape[0]):
        frames = window[:, offset : offset + half_taps].reshape(
            session_rows * half_taps, half_width
        )
        partial_value = partial_value + jnp.dot(
            frames, res_weight[offset], preferred_element_type=jnp.float32
        )
    partial_value = partial_value.reshape(session_rows, half_taps, hidden_width)
    summed = lax.psum(partial_value, "segment")
    hidden = apply_elu(summed + res_bias).astype(jnp.bfloat16)
    projected = jnp.dot(
        hidden.reshape(session_rows * half_taps, hidden_width),
        skip_weight,
        preferred_element_type=jnp.float32,
    )
    decoded_block = upsampled + projected.reshape(session_rows, half_taps, half_width) + skip_bias
    return (decoded_block.astype(jnp.bfloat16), new_tail)


CHUNKS = 4
HALF_TAPS = 8
MESH = pl.DeviceIdType.MESH


def elu32(values):
    return jnp.where(values > 0, values, jnp.exp(jnp.minimum(values, 0.0)) - 1.0)


def fused_kernel(
    lat_ref, w_ref, cache_ref, convb_ref, resw_ref, resb_ref, skipw_ref, skipb_ref,
    dec_ref, tail_ref,
    wbuf, latb, cach, exc, ups, win, resbuf, outbox, match,
    w_send, w_recv, lat_send, lat_recv, hop_send, hop_recv, c_send, c_recv,
    win_send, win_recv, out_send, out_recv, local_sem,
):
    g = lax.axis_index("groups")
    j = lax.axis_index("streams")
    c = lax.axis_index("segment")
    z, x = j // 2, lax.rem(j, 2)
    per = HALF_TAPS // CHUNKS

    def at(gg, jj, cc):
        return {"groups": gg, "streams": jj, "segment": cc}

    def remote(src, dst, ss, rs, dev):
        return pltpu.make_async_remote_copy(
            src_ref=src, dst_ref=dst, send_sem=ss, recv_sem=rs, device_id=dev, device_id_type=MESH
        )

    partner = at(g, j, 1 - c)
    across = at(1 - g, j, c)

    barrier = pltpu.get_barrier_semaphore()
    for d in range(8):
        peer = lax.rem(j + d, 8)
        if d:
            pl.semaphore_signal(barrier, inc=1, device_id=at(g, peer, c), device_id_type=MESH)
        pl.semaphore_signal(barrier, inc=1, device_id=at(1 - g, peer, c), device_id_type=MESH)
    pl.semaphore_signal(barrier, inc=1, device_id=partner, device_id_type=MESH)

    own_lat = pltpu.make_async_copy(
        lat_ref.at[pl.ds(j * 32, 32)], latb.at[g, c, pl.ds(j * 32, 32)], local_sem.at[0]
    )
    own_w = pltpu.make_async_copy(
        w_ref.at[pl.ds(g * HALF_TAPS, HALF_TAPS)], wbuf.at[:, pl.ds(j * 128, 128)], local_sem.at[1]
    )
    own_res = pltpu.make_async_copy(resw_ref, resbuf.at[c], local_sem.at[2])
    own_cache = pltpu.make_async_copy(cache_ref.at[j], cach.at[j], local_sem.at[3])
    own_w.start()
    own_lat.start()
    own_res.start()

    @pl.when(g == 0)
    def _():
        own_cache.start()

    own_w.wait()
    pl.semaphore_wait(barrier, 16)

    def lat_copy(d):
        peer = lax.rem(j + d, 8)
        return remote(
            lat_ref.at[pl.ds(peer * 32, 32)], latb.at[g, c, pl.ds(j * 32, 32)],
            lat_send.at[d], lat_recv.at[d], at(g, peer, c),
        )

    def lat_arrival(d):
        peer = lax.rem(j + 8 - d, 8)
        return remote(
            lat_ref.at[pl.ds(0, 32)], latb.at[g, c, pl.ds(peer * 32, 32)],
            lat_send.at[d], lat_recv.at[d], at(g, peer, c),
        )

    for d in range(1, 8):
        lat_copy(d).start()

    def w_copy(q, piece, slot, dev):
        block = wbuf.at[pl.ds(q * per, per), pl.ds(piece * 128, 128)]
        return remote(block, block, w_send.at[q, slot], w_recv.at[q, slot], dev)

    def up(q, s):
        return w_copy(q, (z - s) * 2 + x, s, at(g, j + 2, c))

    def up_arrival(q, s):
        return w_copy(q, (z - 1 - s) * 2 + x, s, at(g, j - 2, c))

    def down(q, s):
        return w_copy(q, (z + s) * 2 + x, 3 + s, at(g, j - 2, c))

    def down_arrival(q, s):
        return w_copy(q, (z + 1 + s) * 2 + x, 3 + s, at(g, j + 2, c))

    def side(q, p):
        return w_copy(q, p * 2 + x, 6 + p, at(g, z * 2 + 1 - x, c))

    def side_arrival(q, p):
        return w_copy(q, p * 2 + 1 - x, 6 + p, at(g, z * 2 + 1 - x, c))

    for q in range(CHUNKS):

        @pl.when(z < 3)
        def _():
            up(q, 0).start()

        @pl.when(z > 0)
        def _():
            down(q, 0).start()

        side(q, z).start()

    def cache_copy(d):
        peer = lax.rem(j + d, 8)
        return remote(
            cache_ref.at[peer], cach.at[g * 8 + j], c_send.at[d], c_recv.at[g * 8 + d], at(0, peer, c)
        )

    def cache_arrival(gg, d):
        peer = lax.rem(j + 8 - d, 8)
        return remote(
            cache_ref.at[0], cach.at[gg * 8 + peer], c_send.at[d], c_recv.at[gg * 8 + d],
            at(gg, peer, c),
        )

    for d in range(8):
        if d:
            cache_copy(d).start()
        else:

            @pl.when(g == 1)
            def _():
                cache_copy(0).start()

    res_out = remote(resw_ref, resbuf.at[c], hop_send.at[3], hop_recv.at[3], partner)
    res_in = remote(resw_ref, resbuf.at[1 - c], hop_send.at[3], hop_recv.at[3], partner)
    res_out.start()

    def hop(gg, cc, index, dev):
        block = latb.at[gg, cc]
        return remote(block, block, hop_send.at[index], hop_recv.at[index], dev)

    own_lat.wait()
    for d in range(1, 8):
        lat_arrival(d).wait_recv()
    hop(g, c, 1, across).start()
    hop(g, c, 0, partner).start()

    def forward(q):
        for s in range(3):

            @pl.when(z - 1 - s >= 0)
            def _():
                up_arrival(q, s).wait_recv()
                if s < 2:

                    @pl.when(z < 3)
                    def _():
                        up(q, s + 1).start()

                side(q, z - 1 - s).start()

            @pl.when(z + 1 + s <= 3)
            def _():
                down_arrival(q, s).wait_recv()
                if s < 2:

                    @pl.when(z > 0)
                    def _():
                        down(q, s + 1).start()

                side(q, z + 1 + s).start()

    def settle(q):
        for p in range(4):
            side_arrival(q, p).wait_recv()

    hop(1 - g, c, 1, across).wait_recv()
    hop(1 - g, c, 2, partner).start()
    hop(g, 1 - c, 0, partner).wait_recv()
    hop(1 - g, 1 - c, 2, partner).wait_recv()
    forward(0)
    for gg in range(2):
        for h in range(2):
            exc[gg * 256 : (gg + 1) * 256, h * 512 : (h + 1) * 512] = elu32(
                latb[gg, h].astype(jnp.float32)
            ).astype(jnp.bfloat16)

    def win_copy(i):
        return remote(win.at[c, i], win.at[c, i], win_send.at[i], win_recv.at[i], partner)

    def win_arrival(i):
        return remote(win.at[1 - c, i], win.at[1 - c, i], win_send.at[i], win_recv.at[i], partner)

    def placed(gg, row):
        lanes = lax.broadcasted_iota(jnp.int32, (256, 128), 1)
        chosen = jnp.where(lax.rem(lanes, 16) == row, match[gg], 0.0).astype(jnp.bfloat16)
        rows = cach[gg * 8 : (gg + 1) * 8, 0:16].reshape(128, 256)
        return jnp.dot(chosen, rows, preferred_element_type=jnp.float32)

    own_res.wait()
    res_in.wait_recv()

    @pl.when(g == 0)
    def _():
        own_cache.wait()
        for gg in range(2):
            for d in range(8):
                if gg or d:
                    cache_arrival(gg, d).wait_recv()
        for gg in range(2):
            slots = cach[gg * 8 : (gg + 1) * 8, 16:32].reshape(128, 256).astype(jnp.float32)
            sessions = lax.broadcasted_iota(jnp.int32, (128, 256), 1).astype(jnp.float32)
            match[gg] = jnp.where(slots == sessions, 1.0, 0.0).T
            for i in range(2):
                win[c, i, gg * 256 : (gg + 1) * 256] = placed(gg, 8 + i).astype(jnp.bfloat16)
        for i in range(2):
            win_copy(i).start()

    def spread_of(gg, t):
        return jnp.dot(exc[gg * 256 : (gg + 1) * 256], wbuf[t], preferred_element_type=jnp.float32)

    def dec_out(t):
        return remote(outbox.at[t], dec_ref.at[t], out_send.at[t], out_recv.at[t], across)

    def tail_out(t):
        return remote(outbox.at[t], tail_ref.at[t], out_send.at[t], out_recv.at[t], across)

    def upsample(t):
        for gg in range(2):
            value = spread_of(gg, t) + placed(gg, t) + convb_ref[...]
            ups[t, gg * 256 : (gg + 1) * 256] = value
            win[c, t + 2, gg * 256 : (gg + 1) * 256] = elu32(value).astype(jnp.bfloat16)
        win_copy(t + 2).start()

    def decode(t):
        win_arrival(t + 2).wait_recv()
        for gg in (1, 0):
            part = slice(gg * 256, (gg + 1) * 256)
            branch = jnp.zeros((256, 256), jnp.float32) + resb_ref[...]
            for k in range(3):
                for h in range(2):
                    branch = branch + jnp.dot(
                        win[h, t + k, part], resbuf[h, k], preferred_element_type=jnp.float32
                    )
            hidden = elu32(branch).astype(jnp.bfloat16)
            value = ups[t, part] + jnp.dot(
                hidden, skipw_ref[...], preferred_element_type=jnp.float32
            ) + skipb_ref[...]
            if gg:
                outbox[t] = value.astype(jnp.bfloat16)
                dec_out(t).start()
            else:
                dec_ref[t] = value.astype(jnp.bfloat16)

    def work(q):
        @pl.when(g == 0)
        def _():
            @pl.loop(q * per, (q + 1) * per)
            def _(t):
                upsample(t)

                @pl.when(t == 0)
                def _():
                    win_arrival(0).wait_recv()
                    win_arrival(1).wait_recv()

                @pl.when(t > 0)
                def _():
                    decode(t - 1)

        @pl.when(g == 1)
        def _():
            @pl.loop(q * per, (q + 1) * per)
            def _(t):
                outbox[t] = spread_of(0, t).astype(jnp.bfloat16)
                tail_out(t).start()
                tail_ref[t] = spread_of(1, t).astype(jnp.bfloat16)

    for q in range(CHUNKS):
        if q + 1 < CHUNKS:
            forward(q + 1)
        settle(q)
        work(q)

    @pl.when(g == 0)
    def _():
        decode(HALF_TAPS - 1)
        for t in range(HALF_TAPS):
            dec_out(t).wait_send()
            tail_out(t).wait_recv()
        for i in range(HALF_TAPS + 2):
            win_copy(i).wait_send()

    @pl.when(g == 1)
    def _():
        for t in range(HALF_TAPS):
            tail_out(t).wait_send()
            dec_out(t).wait_recv()
        cache_copy(0).wait_send()

    for d in range(1, 8):
        lat_copy(d).wait_send()
        cache_copy(d).wait_send()
    res_out.wait_send()
    hop(g, c, 0, partner).wait_send()
    hop(g, c, 1, across).wait_send()
    hop(1 - g, c, 2, partner).wait_send()
    for q in range(CHUNKS):
        for s in range(3):

            @pl.when((z < 3) & (z - s >= 0))
            def _():
                up(q, s).wait_send()

            @pl.when((z > 0) & (z + s <= 3))
            def _():
                down(q, s).wait_send()

        for p in range(4):
            side(q, p).wait_send()


def fused(
    latent, conv_weight, conv_bias, tail_cache, input_cache, resume_slot,
    res_weight, res_bias, skip_weight, skip_bias,
):
    taps_first = conv_weight.transpose(1, 0, 2)
    slots = jnp.broadcast_to(resume_slot.astype(jnp.bfloat16)[:, None, None], (8, 16, 256))
    packed = jnp.concatenate(
        [tail_cache, input_cache, jnp.zeros((8, 6, 256), jnp.bfloat16), slots], axis=1
    )
    dma = pltpu.SemaphoreType.DMA
    bf16, f32 = jnp.bfloat16, jnp.float32
    decoded, new_tail = pl.pallas_call(
        fused_kernel,
        out_shape=(
            jax.ShapeDtypeStruct((8, 256, 256), bf16),
            jax.ShapeDtypeStruct((8, 256, 256), bf16),
        ),
        in_specs=[pl.BlockSpec(memory_space=pltpu.VMEM)] * 8,
        out_specs=(pl.BlockSpec(memory_space=pltpu.VMEM),) * 2,
        scratch_shapes=[
            pltpu.VMEM((8, 1024, 256), bf16),
            pltpu.VMEM((2, 2, 256, 512), bf16),
            pltpu.VMEM((16, 32, 256), bf16),
            pltpu.VMEM((512, 1024), bf16),
            pltpu.VMEM((8, 512, 256), f32),
            pltpu.VMEM((2, 10, 512, 256), bf16),
            pltpu.VMEM((2, 3, 256, 256), bf16),
            pltpu.VMEM((8, 256, 256), bf16),
            pltpu.VMEM((2, 256, 128), f32),
            dma((CHUNKS, 10)), dma((CHUNKS, 10)),
            dma((8,)), dma((8,)),
            dma((4,)), dma((4,)),
            dma((8,)), dma((16,)),
            dma((10,)), dma((10,)),
            dma((8,)), dma((8,)),
            dma((4,)),
        ],
        compiler_params=pltpu.CompilerParams(
            collective_id=0, has_side_effects=True, vmem_limit_bytes=48 * 1024 * 1024
        ),
    )(
        latent, taps_first, packed, conv_bias[None, :], res_weight, res_bias[None, :],
        skip_weight, skip_bias[None, :],
    )
    return decoded.transpose(1, 0, 2), new_tail.transpose(1, 0, 2)


def solution(mesh):
    sizes = tuple(mesh.shape[name] for name in ("groups", "streams", "segment"))
    body = fused if sizes == (2, 8, 2) else local
    placed = (
        P(("groups", "streams"), "segment"),
        P("streams", None, "segment"),
        P("segment"),
        P(("groups", "streams"), None, "segment"),
        P(("groups", "streams"), None, "segment"),
        P(("groups", "streams")),
        P(None, "segment", None),
        P(),
        P(None, "segment"),
        P("segment"),
    )
    return jax.shard_map(
        body,
        mesh=mesh,
        in_specs=placed,
        out_specs=(
            P(("groups", "streams"), None, "segment"),
            P(("groups", "streams"), None, "segment"),
        ),
        check_vma=False,
    )
```

```python
import jax
import jax.numpy as jnp
from jax import lax
from jax.experimental import pallas as pl
from jax.experimental.pallas import tpu as pltpu
from jax.sharding import PartitionSpec as P


def apply_elu(values):
    return jnp.where(values > 0, values, jnp.expm1(jnp.minimum(values, 0.0)))


def local(
    latent,
    conv_weight,
    conv_bias,
    tail_cache,
    input_cache,
    resume_slot,
    res_weight,
    res_bias,
    skip_weight,
    skip_bias,
):
    handed = lax.all_to_all(latent, "streams", split_axis=0, concat_axis=0, tiled=True)
    excitation_half = apply_elu(handed.astype(jnp.float32)).astype(jnp.bfloat16)
    excitation = lax.all_gather(excitation_half, "segment", axis=1, tiled=True)
    session_rows = excitation.shape[0]
    tap_count = conv_weight.shape[1]
    half_taps = tap_count // 2
    half_width = conv_weight.shape[2]
    piece = lax.all_gather(conv_weight, "streams", axis=0, tiled=True)
    kernel_rows = piece.reshape(piece.shape[0], tap_count * half_width)
    spread = jnp.dot(excitation, kernel_rows, preferred_element_type=jnp.float32)
    spread = spread.reshape(session_rows, tap_count, half_width)
    fetched_tail, fetched_input, fetched_slot = (
        lax.all_to_all(tail_cache, "streams", split_axis=0, concat_axis=0, tiled=True),
        lax.all_to_all(input_cache, "streams", split_axis=0, concat_axis=0, tiled=True),
        lax.all_to_all(resume_slot, "streams", split_axis=0, concat_axis=0, tiled=True),
    )
    arrivals = fetched_slot.shape[0]
    state_steps = fetched_input.shape[1]
    packed = jnp.concatenate(
        [fetched_tail.reshape(arrivals, -1), fetched_input.reshape(arrivals, -1)], axis=1
    )
    one_hot = (fetched_slot[None, :] == jnp.arange(session_rows, dtype=jnp.int32)[:, None]).astype(
        jnp.bfloat16
    )
    placed = jnp.dot(one_hot, packed, preferred_element_type=jnp.float32)
    prev_tail = placed[:, : half_taps * half_width].reshape(session_rows, half_taps, half_width)
    prev_input = (
        placed[:, half_taps * half_width :]
        .reshape(session_rows, state_steps, half_width)
        .astype(jnp.bfloat16)
    )
    upsampled = spread[:, :half_taps] + prev_tail + conv_bias
    new_tail = spread[:, half_taps:].astype(jnp.bfloat16)
    excited = apply_elu(upsampled).astype(jnp.bfloat16)
    window = jnp.concatenate([prev_input, excited], axis=1)
    hidden_width = res_weight.shape[2]
    partial_value = jnp.zeros((session_rows * half_taps, hidden_width), jnp.float32)
    for offset in range(res_weight.shape[0]):
        frames = window[:, offset : offset + half_taps].reshape(
            session_rows * half_taps, half_width
        )
        partial_value = partial_value + jnp.dot(
            frames, res_weight[offset], preferred_element_type=jnp.float32
        )
    partial_value = partial_value.reshape(session_rows, half_taps, hidden_width)
    summed = lax.psum(partial_value, "segment")
    hidden = apply_elu(summed + res_bias).astype(jnp.bfloat16)
    projected = jnp.dot(
        hidden.reshape(session_rows * half_taps, hidden_width),
        skip_weight,
        preferred_element_type=jnp.float32,
    )
    decoded_block = upsampled + projected.reshape(session_rows, half_taps, half_width) + skip_bias
    return (decoded_block.astype(jnp.bfloat16), new_tail)


CHUNKS = 8
Z_AHEAD = 2
X_AHEAD = 3
HALF_TAPS = 8
MESH = pl.DeviceIdType.MESH


def elu32(values):
    return jnp.where(values > 0, values, jnp.exp(jnp.minimum(values, 0.0)) - 1.0)


def fused_kernel(
    lat_ref, w_ref, cache_ref, convb_ref, resw_ref, resb_ref, skipw_ref, skipb_ref,
    dec_ref, tail_ref,
    wbuf, latb, cach, exc, ups, win, resbuf, outbox, match,
    w_send, w_recv, lat_send, lat_recv, hop_send, hop_recv, c_send, c_recv,
    win_send, win_recv, out_send, out_recv, local_sem,
):
    g = lax.axis_index("groups")
    j = lax.axis_index("streams")
    c = lax.axis_index("segment")
    z, x = j // 2, lax.rem(j, 2)
    per = HALF_TAPS // CHUNKS

    def at(gg, jj, cc):
        return {"groups": gg, "streams": jj, "segment": cc}

    def remote(src, dst, ss, rs, dev):
        return pltpu.make_async_remote_copy(
            src_ref=src, dst_ref=dst, send_sem=ss, recv_sem=rs, device_id=dev, device_id_type=MESH
        )

    partner = at(g, j, 1 - c)
    across = at(1 - g, j, c)

    barrier = pltpu.get_barrier_semaphore()
    for d in range(8):
        peer = lax.rem(j + d, 8)
        if d:
            pl.semaphore_signal(barrier, inc=1, device_id=at(g, peer, c), device_id_type=MESH)
        pl.semaphore_signal(barrier, inc=1, device_id=at(1 - g, peer, c), device_id_type=MESH)
    pl.semaphore_signal(barrier, inc=1, device_id=partner, device_id_type=MESH)

    own_lat = pltpu.make_async_copy(
        lat_ref.at[pl.ds(j * 32, 32)], latb.at[g, c, pl.ds(j * 32, 32)], local_sem.at[0]
    )
    own_w = pltpu.make_async_copy(
        w_ref.at[pl.ds(g * HALF_TAPS, HALF_TAPS)], wbuf.at[:, pl.ds(j * 128, 128)], local_sem.at[1]
    )
    own_res = pltpu.make_async_copy(resw_ref, resbuf.at[c], local_sem.at[2])
    own_cache = pltpu.make_async_copy(cache_ref.at[j], cach.at[j], local_sem.at[3])
    own_w.start()
    own_lat.start()
    own_res.start()

    @pl.when(g == 0)
    def _():
        own_cache.start()

    own_w.wait()
    pl.semaphore_wait(barrier, 16)

    def lat_copy(d):
        peer = lax.rem(j + d, 8)
        return remote(
            lat_ref.at[pl.ds(peer * 32, 32)], latb.at[g, c, pl.ds(j * 32, 32)],
            lat_send.at[d], lat_recv.at[d], at(g, peer, c),
        )

    def lat_arrival(d):
        peer = lax.rem(j + 8 - d, 8)
        return remote(
            lat_ref.at[pl.ds(0, 32)], latb.at[g, c, pl.ds(peer * 32, 32)],
            lat_send.at[d], lat_recv.at[d], at(g, peer, c),
        )

    for d in range(1, 8):
        lat_copy(d).start()

    def w_copy(q, piece, slot, dev):
        block = wbuf.at[pl.ds(q * per, per), pl.ds(piece * 128, 128)]
        return remote(block, block, w_send.at[q, slot], w_recv.at[q, slot], dev)

    def up(q, s):
        return w_copy(q, (z - s) * 2 + x, s, at(g, j + 2, c))

    def up_arrival(q, s):
        return w_copy(q, (z - 1 - s) * 2 + x, s, at(g, j - 2, c))

    def down(q, s):
        return w_copy(q, (z + s) * 2 + x, 3 + s, at(g, j - 2, c))

    def down_arrival(q, s):
        return w_copy(q, (z + 1 + s) * 2 + x, 3 + s, at(g, j + 2, c))

    def side(q, p):
        return w_copy(q, p * 2 + x, 6 + p, at(g, z * 2 + 1 - x, c))

    def side_arrival(q, p):
        return w_copy(q, p * 2 + 1 - x, 6 + p, at(g, z * 2 + 1 - x, c))

    def own_z(q):
        @pl.when(z < 3)
        def _():
            up(q, 0).start()

        @pl.when(z > 0)
        def _():
            down(q, 0).start()

    for q in range(X_AHEAD):
        if q < Z_AHEAD:
            own_z(q)
        side(q, z).start()

    def cache_copy(d):
        peer = lax.rem(j + d, 8)
        return remote(
            cache_ref.at[peer], cach.at[g * 8 + j], c_send.at[d], c_recv.at[g * 8 + d], at(0, peer, c)
        )

    def cache_arrival(gg, d):
        peer = lax.rem(j + 8 - d, 8)
        return remote(
            cache_ref.at[0], cach.at[gg * 8 + peer], c_send.at[d], c_recv.at[gg * 8 + d],
            at(gg, peer, c),
        )

    for d in range(8):
        if d:
            cache_copy(d).start()
        else:

            @pl.when(g == 1)
            def _():
                cache_copy(0).start()

    res_out = remote(resw_ref, resbuf.at[c], hop_send.at[3], hop_recv.at[3], partner)
    res_in = remote(resw_ref, resbuf.at[1 - c], hop_send.at[3], hop_recv.at[3], partner)
    res_out.start()

    def hop(gg, cc, index, dev):
        block = latb.at[gg, cc]
        return remote(block, block, hop_send.at[index], hop_recv.at[index], dev)

    own_lat.wait()
    for d in range(1, 8):
        lat_arrival(d).wait_recv()
    hop(g, c, 1, across).start()
    hop(g, c, 0, partner).start()

    def forward(q, s):
        @pl.when(z - 1 - s >= 0)
        def _():
            up_arrival(q, s).wait_recv()
            if s < 2:

                @pl.when(z < 3)
                def _():
                    up(q, s + 1).start()

            side(q, z - 1 - s).start()

        @pl.when(z + 1 + s <= 3)
        def _():
            down_arrival(q, s).wait_recv()
            if s < 2:

                @pl.when(z > 0)
                def _():
                    down(q, s + 1).start()

            side(q, z + 1 + s).start()

    def pump(i):
        for s in (2, 1, 0):
            q = i - s
            if isinstance(q, int):
                if q >= 0:
                    forward(q, s)
            else:

                @pl.when(q < CHUNKS)
                def _():
                    forward(q, s)

        @pl.when(i + Z_AHEAD < CHUNKS)
        def _():
            own_z(i + Z_AHEAD)

        @pl.when(i + X_AHEAD < CHUNKS)
        def _():
            side(i + X_AHEAD, z).start()

    def settle(q):
        for p in range(4):
            side_arrival(q, p).wait_recv()

    pump(0)
    hop(1 - g, c, 1, across).wait_recv()
    hop(1 - g, c, 2, partner).start()
    pump(1)
    hop(g, 1 - c, 0, partner).wait_recv()
    hop(1 - g, 1 - c, 2, partner).wait_recv()
    for gg in range(2):
        for h in range(2):
            exc[gg * 256 : (gg + 1) * 256, h * 512 : (h + 1) * 512] = elu32(
                latb[gg, h].astype(jnp.float32)
            ).astype(jnp.bfloat16)

    def win_copy(i):
        return remote(win.at[c, i], win.at[c, i], win_send.at[i], win_recv.at[i], partner)

    def win_arrival(i):
        return remote(win.at[1 - c, i], win.at[1 - c, i], win_send.at[i], win_recv.at[i], partner)

    def placed(gg, row):
        lanes = lax.broadcasted_iota(jnp.int32, (256, 128), 1)
        chosen = jnp.where(lax.rem(lanes, 16) == row, match[gg], 0.0).astype(jnp.bfloat16)
        rows = cach[gg * 8 : (gg + 1) * 8, 0:16].reshape(128, 256)
        return jnp.dot(chosen, rows, preferred_element_type=jnp.float32)

    pump(2)
    own_res.wait()
    res_in.wait_recv()

    @pl.when(g == 0)
    def _():
        own_cache.wait()
        for gg in range(2):
            for d in range(8):
                if gg or d:
                    cache_arrival(gg, d).wait_recv()
        for gg in range(2):
            slots = cach[gg * 8 : (gg + 1) * 8, 16:32].reshape(128, 256).astype(jnp.float32)
            sessions = lax.broadcasted_iota(jnp.int32, (128, 256), 1).astype(jnp.float32)
            match[gg] = jnp.where(slots == sessions, 1.0, 0.0).T
            for i in range(2):
                win[c, i, gg * 256 : (gg + 1) * 256] = placed(gg, 8 + i).astype(jnp.bfloat16)
        for i in range(2):
            win_copy(i).start()

    def spread_of(gg, t):
        return jnp.dot(exc[gg * 256 : (gg + 1) * 256], wbuf[t], preferred_element_type=jnp.float32)

    def dec_out(t):
        return remote(outbox.at[t], dec_ref.at[t], out_send.at[t], out_recv.at[t], across)

    def tail_out(t):
        return remote(outbox.at[t], tail_ref.at[t], out_send.at[t], out_recv.at[t], across)

    def upsample(t):
        for gg in range(2):
            value = spread_of(gg, t) + placed(gg, t) + convb_ref[...]
            ups[t, gg * 256 : (gg + 1) * 256] = value
            win[c, t + 2, gg * 256 : (gg + 1) * 256] = elu32(value).astype(jnp.bfloat16)
        win_copy(t + 2).start()

    def decode(t):
        win_arrival(t + 2).wait_recv()
        for gg in (1, 0):
            part = slice(gg * 256, (gg + 1) * 256)
            branch = jnp.zeros((256, 256), jnp.float32) + resb_ref[...]
            for k in range(3):
                for h in range(2):
                    branch = branch + jnp.dot(
                        win[h, t + k, part], resbuf[h, k], preferred_element_type=jnp.float32
                    )
            hidden = elu32(branch).astype(jnp.bfloat16)
            value = ups[t, part] + jnp.dot(
                hidden, skipw_ref[...], preferred_element_type=jnp.float32
            ) + skipb_ref[...]
            if gg:
                outbox[t] = value.astype(jnp.bfloat16)
                dec_out(t).start()
            else:
                dec_ref[t] = value.astype(jnp.bfloat16)

    def work(t):
        @pl.when(g == 0)
        def _():
            upsample(t)

            @pl.when(t == 0)
            def _():
                win_arrival(0).wait_recv()
                win_arrival(1).wait_recv()

            @pl.when(t > 0)
            def _():
                decode(t - 1)

        @pl.when(g == 1)
        def _():
            outbox[t] = spread_of(0, t).astype(jnp.bfloat16)
            tail_out(t).start()
            tail_ref[t] = spread_of(1, t).astype(jnp.bfloat16)

    @pl.loop(3, CHUNKS + 3)
    def _(i):
        pump(i)
        settle(i - 3)
        work(i - 3)

    @pl.when(g == 0)
    def _():
        decode(HALF_TAPS - 1)
        for t in range(HALF_TAPS):
            dec_out(t).wait_send()
            tail_out(t).wait_recv()
        for i in range(HALF_TAPS + 2):
            win_copy(i).wait_send()

    @pl.when(g == 1)
    def _():
        for t in range(HALF_TAPS):
            tail_out(t).wait_send()
            dec_out(t).wait_recv()
        cache_copy(0).wait_send()

    for d in range(1, 8):
        lat_copy(d).wait_send()
        cache_copy(d).wait_send()
    res_out.wait_send()
    hop(g, c, 0, partner).wait_send()
    hop(g, c, 1, across).wait_send()
    hop(1 - g, c, 2, partner).wait_send()
    @pl.loop(0, CHUNKS)
    def _(q):
        for s in range(3):

            @pl.when((z < 3) & (z - s >= 0))
            def _():
                up(q, s).wait_send()

            @pl.when((z > 0) & (z + s <= 3))
            def _():
                down(q, s).wait_send()

        for p in range(4):
            side(q, p).wait_send()


def fused(
    latent, conv_weight, conv_bias, tail_cache, input_cache, resume_slot,
    res_weight, res_bias, skip_weight, skip_bias,
):
    taps_first = conv_weight.transpose(1, 0, 2)
    slots = jnp.broadcast_to(resume_slot.astype(jnp.bfloat16)[:, None, None], (8, 16, 256))
    packed = jnp.concatenate(
        [tail_cache, input_cache, jnp.zeros((8, 6, 256), jnp.bfloat16), slots], axis=1
    )
    dma = pltpu.SemaphoreType.DMA
    bf16, f32 = jnp.bfloat16, jnp.float32
    decoded, new_tail = pl.pallas_call(
        fused_kernel,
        out_shape=(
            jax.ShapeDtypeStruct((8, 256, 256), bf16),
            jax.ShapeDtypeStruct((8, 256, 256), bf16),
        ),
        in_specs=[pl.BlockSpec(memory_space=pltpu.VMEM)] * 8,
        out_specs=(pl.BlockSpec(memory_space=pltpu.VMEM),) * 2,
        scratch_shapes=[
            pltpu.VMEM((8, 1024, 256), bf16),
            pltpu.VMEM((2, 2, 256, 512), bf16),
            pltpu.VMEM((16, 32, 256), bf16),
            pltpu.VMEM((512, 1024), bf16),
            pltpu.VMEM((8, 512, 256), f32),
            pltpu.VMEM((2, 10, 512, 256), bf16),
            pltpu.VMEM((2, 3, 256, 256), bf16),
            pltpu.VMEM((8, 256, 256), bf16),
            pltpu.VMEM((2, 256, 128), f32),
            dma((CHUNKS, 10)), dma((CHUNKS, 10)),
            dma((8,)), dma((8,)),
            dma((4,)), dma((4,)),
            dma((8,)), dma((16,)),
            dma((10,)), dma((10,)),
            dma((8,)), dma((8,)),
            dma((4,)),
        ],
        compiler_params=pltpu.CompilerParams(
            collective_id=0, has_side_effects=True, vmem_limit_bytes=48 * 1024 * 1024
        ),
    )(
        latent, taps_first, packed, conv_bias[None, :], res_weight, res_bias[None, :],
        skip_weight, skip_bias[None, :],
    )
    return decoded.transpose(1, 0, 2), new_tail.transpose(1, 0, 2)


def solution(mesh):
    sizes = tuple(mesh.shape[name] for name in ("groups", "streams", "segment"))
    body = fused if sizes == (2, 8, 2) else local
    placed = (
        P(("groups", "streams"), "segment"),
        P("streams", None, "segment"),
        P("segment"),
        P(("groups", "streams"), None, "segment"),
        P(("groups", "streams"), None, "segment"),
        P(("groups", "streams")),
        P(None, "segment", None),
        P(),
        P(None, "segment"),
        P("segment"),
    )
    return jax.shard_map(
        body,
        mesh=mesh,
        in_specs=placed,
        out_specs=(
            P(("groups", "streams"), None, "segment"),
            P(("groups", "streams"), None, "segment"),
        ),
        check_vma=False,
    )
```

```python
import jax
import jax.numpy as jnp
from jax import lax
from jax.experimental import pallas as pl
from jax.experimental.pallas import tpu as pltpu
from jax.sharding import PartitionSpec as P


def apply_elu(values):
    return jnp.where(values > 0, values, jnp.expm1(jnp.minimum(values, 0.0)))


def local(
    latent,
    conv_weight,
    conv_bias,
    tail_cache,
    input_cache,
    resume_slot,
    res_weight,
    res_bias,
    skip_weight,
    skip_bias,
):
    handed = lax.all_to_all(latent, "streams", split_axis=0, concat_axis=0, tiled=True)
    excitation_half = apply_elu(handed.astype(jnp.float32)).astype(jnp.bfloat16)
    excitation = lax.all_gather(excitation_half, "segment", axis=1, tiled=True)
    session_rows = excitation.shape[0]
    tap_count = conv_weight.shape[1]
    half_taps = tap_count // 2
    half_width = conv_weight.shape[2]
    piece = lax.all_gather(conv_weight, "streams", axis=0, tiled=True)
    kernel_rows = piece.reshape(piece.shape[0], tap_count * half_width)
    spread = jnp.dot(excitation, kernel_rows, preferred_element_type=jnp.float32)
    spread = spread.reshape(session_rows, tap_count, half_width)
    fetched_tail, fetched_input, fetched_slot = (
        lax.all_to_all(tail_cache, "streams", split_axis=0, concat_axis=0, tiled=True),
        lax.all_to_all(input_cache, "streams", split_axis=0, concat_axis=0, tiled=True),
        lax.all_to_all(resume_slot, "streams", split_axis=0, concat_axis=0, tiled=True),
    )
    arrivals = fetched_slot.shape[0]
    state_steps = fetched_input.shape[1]
    packed = jnp.concatenate(
        [fetched_tail.reshape(arrivals, -1), fetched_input.reshape(arrivals, -1)], axis=1
    )
    one_hot = (fetched_slot[None, :] == jnp.arange(session_rows, dtype=jnp.int32)[:, None]).astype(
        jnp.bfloat16
    )
    placed = jnp.dot(one_hot, packed, preferred_element_type=jnp.float32)
    prev_tail = placed[:, : half_taps * half_width].reshape(session_rows, half_taps, half_width)
    prev_input = (
        placed[:, half_taps * half_width :]
        .reshape(session_rows, state_steps, half_width)
        .astype(jnp.bfloat16)
    )
    upsampled = spread[:, :half_taps] + prev_tail + conv_bias
    new_tail = spread[:, half_taps:].astype(jnp.bfloat16)
    excited = apply_elu(upsampled).astype(jnp.bfloat16)
    window = jnp.concatenate([prev_input, excited], axis=1)
    hidden_width = res_weight.shape[2]
    partial_value = jnp.zeros((session_rows * half_taps, hidden_width), jnp.float32)
    for offset in range(res_weight.shape[0]):
        frames = window[:, offset : offset + half_taps].reshape(
            session_rows * half_taps, half_width
        )
        partial_value = partial_value + jnp.dot(
            frames, res_weight[offset], preferred_element_type=jnp.float32
        )
    partial_value = partial_value.reshape(session_rows, half_taps, hidden_width)
    summed = lax.psum(partial_value, "segment")
    hidden = apply_elu(summed + res_bias).astype(jnp.bfloat16)
    projected = jnp.dot(
        hidden.reshape(session_rows * half_taps, hidden_width),
        skip_weight,
        preferred_element_type=jnp.float32,
    )
    decoded_block = upsampled + projected.reshape(session_rows, half_taps, half_width) + skip_bias
    return (decoded_block.astype(jnp.bfloat16), new_tail)


CHUNKS = 8
Z_AHEAD = 4
X_AHEAD = 6
HALF_TAPS = 8
MESH = pl.DeviceIdType.MESH


def elu32(values):
    return jnp.where(values > 0, values, jnp.exp(jnp.minimum(values, 0.0)) - 1.0)


def fused_kernel(
    lat_ref, w_ref, cache_ref, convb_ref, resw_ref, resb_ref, skipw_ref, skipb_ref,
    dec_ref, tail_ref,
    wbuf, latb, cach, exc, ups, win, resbuf, outbox, match,
    w_send, w_recv, lat_send, lat_recv, hop_send, hop_recv, c_send, c_recv,
    win_send, win_recv, out_send, out_recv, local_sem,
):
    g = lax.axis_index("groups")
    j = lax.axis_index("streams")
    c = lax.axis_index("segment")
    z, x = j // 2, lax.rem(j, 2)
    per = HALF_TAPS // CHUNKS

    def at(gg, jj, cc):
        return {"groups": gg, "streams": jj, "segment": cc}

    def remote(src, dst, ss, rs, dev):
        return pltpu.make_async_remote_copy(
            src_ref=src, dst_ref=dst, send_sem=ss, recv_sem=rs, device_id=dev, device_id_type=MESH
        )

    partner = at(g, j, 1 - c)
    across = at(1 - g, j, c)

    barrier = pltpu.get_barrier_semaphore()
    for d in range(8):
        peer = lax.rem(j + d, 8)
        if d:
            pl.semaphore_signal(barrier, inc=1, device_id=at(g, peer, c), device_id_type=MESH)
        pl.semaphore_signal(barrier, inc=1, device_id=at(1 - g, peer, c), device_id_type=MESH)
    pl.semaphore_signal(barrier, inc=1, device_id=partner, device_id_type=MESH)

    own_lat = pltpu.make_async_copy(
        lat_ref.at[pl.ds(j * 32, 32)], latb.at[g, c, pl.ds(j * 32, 32)], local_sem.at[0]
    )
    own_w = pltpu.make_async_copy(
        w_ref.at[pl.ds(g * HALF_TAPS, HALF_TAPS)], wbuf.at[:, pl.ds(j * 128, 128)], local_sem.at[1]
    )
    own_res = pltpu.make_async_copy(resw_ref, resbuf.at[c], local_sem.at[2])
    own_cache = pltpu.make_async_copy(cache_ref.at[j], cach.at[j], local_sem.at[3])
    own_w.start()
    own_lat.start()
    own_res.start()

    @pl.when(g == 0)
    def _():
        own_cache.start()

    own_w.wait()
    pl.semaphore_wait(barrier, 16)

    def lat_copy(d):
        peer = lax.rem(j + d, 8)
        return remote(
            lat_ref.at[pl.ds(peer * 32, 32)], latb.at[g, c, pl.ds(j * 32, 32)],
            lat_send.at[d], lat_recv.at[d], at(g, peer, c),
        )

    def lat_arrival(d):
        peer = lax.rem(j + 8 - d, 8)
        return remote(
            lat_ref.at[pl.ds(0, 32)], latb.at[g, c, pl.ds(peer * 32, 32)],
            lat_send.at[d], lat_recv.at[d], at(g, peer, c),
        )

    for d in range(1, 8):
        lat_copy(d).start()

    def w_copy(q, piece, slot, dev):
        block = wbuf.at[pl.ds(q * per, per), pl.ds(piece * 128, 128)]
        return remote(block, block, w_send.at[q, slot], w_recv.at[q, slot], dev)

    def up(q, s):
        return w_copy(q, (z - s) * 2 + x, s, at(g, j + 2, c))

    def up_arrival(q, s):
        return w_copy(q, (z - 1 - s) * 2 + x, s, at(g, j - 2, c))

    def down(q, s):
        return w_copy(q, (z + s) * 2 + x, 3 + s, at(g, j - 2, c))

    def down_arrival(q, s):
        return w_copy(q, (z + 1 + s) * 2 + x, 3 + s, at(g, j + 2, c))

    def side(q, p):
        return w_copy(q, p * 2 + x, 6 + p, at(g, z * 2 + 1 - x, c))

    def side_arrival(q, p):
        return w_copy(q, p * 2 + 1 - x, 6 + p, at(g, z * 2 + 1 - x, c))

    def own_z(q):
        @pl.when(z < 3)
        def _():
            up(q, 0).start()

        @pl.when(z > 0)
        def _():
            down(q, 0).start()

    for q in range(X_AHEAD):
        if q < Z_AHEAD:
            own_z(q)
        side(q, z).start()

    def cache_copy(d):
        peer = lax.rem(j + d, 8)
        return remote(
            cache_ref.at[peer], cach.at[g * 8 + j], c_send.at[d], c_recv.at[g * 8 + d], at(0, peer, c)
        )

    def cache_arrival(gg, d):
        peer = lax.rem(j + 8 - d, 8)
        return remote(
            cache_ref.at[0], cach.at[gg * 8 + peer], c_send.at[d], c_recv.at[gg * 8 + d],
            at(gg, peer, c),
        )

    for d in range(8):
        if d:
            cache_copy(d).start()
        else:

            @pl.when(g == 1)
            def _():
                cache_copy(0).start()

    res_out = remote(resw_ref, resbuf.at[c], hop_send.at[3], hop_recv.at[3], partner)
    res_in = remote(resw_ref, resbuf.at[1 - c], hop_send.at[3], hop_recv.at[3], partner)
    res_out.start()

    def hop(gg, cc, index, dev):
        block = latb.at[gg, cc]
        return remote(block, block, hop_send.at[index], hop_recv.at[index], dev)

    own_lat.wait()
    for d in range(1, 8):
        lat_arrival(d).wait_recv()
    hop(g, c, 1, across).start()
    hop(g, c, 0, partner).start()

    def forward(q, s):
        @pl.when(z - 1 - s >= 0)
        def _():
            up_arrival(q, s).wait_recv()
            if s < 2:

                @pl.when(z < 3)
                def _():
                    up(q, s + 1).start()

            side(q, z - 1 - s).start()

        @pl.when(z + 1 + s <= 3)
        def _():
            down_arrival(q, s).wait_recv()
            if s < 2:

                @pl.when(z > 0)
                def _():
                    down(q, s + 1).start()

            side(q, z + 1 + s).start()

    def pump(i):
        for s in (2, 1, 0):
            q = i - s
            if isinstance(q, int):
                if q >= 0:
                    forward(q, s)
            else:

                @pl.when(q < CHUNKS)
                def _():
                    forward(q, s)

        @pl.when(i + Z_AHEAD < CHUNKS)
        def _():
            own_z(i + Z_AHEAD)

        @pl.when(i + X_AHEAD < CHUNKS)
        def _():
            side(i + X_AHEAD, z).start()

    def settle(q):
        for p in range(4):
            side_arrival(q, p).wait_recv()

    pump(0)
    hop(1 - g, c, 1, across).wait_recv()
    hop(1 - g, c, 2, partner).start()
    pump(1)
    hop(g, 1 - c, 0, partner).wait_recv()
    hop(1 - g, 1 - c, 2, partner).wait_recv()
    for gg in range(2):
        for h in range(2):
            exc[gg * 256 : (gg + 1) * 256, h * 512 : (h + 1) * 512] = elu32(
                latb[gg, h].astype(jnp.float32)
            ).astype(jnp.bfloat16)

    def win_copy(i):
        return remote(win.at[c, i], win.at[c, i], win_send.at[i], win_recv.at[i], partner)

    def win_arrival(i):
        return remote(win.at[1 - c, i], win.at[1 - c, i], win_send.at[i], win_recv.at[i], partner)

    def placed(gg, row):
        lanes = lax.broadcasted_iota(jnp.int32, (256, 128), 1)
        chosen = jnp.where(lax.rem(lanes, 16) == row, match[gg], 0.0).astype(jnp.bfloat16)
        rows = cach[gg * 8 : (gg + 1) * 8, 0:16].reshape(128, 256)
        return jnp.dot(chosen, rows, preferred_element_type=jnp.float32)

    pump(2)
    own_res.wait()
    res_in.wait_recv()

    @pl.when(g == 0)
    def _():
        own_cache.wait()
        for gg in range(2):
            for d in range(8):
                if gg or d:
                    cache_arrival(gg, d).wait_recv()
        for gg in range(2):
            slots = cach[gg * 8 : (gg + 1) * 8, 16:32].reshape(128, 256).astype(jnp.float32)
            sessions = lax.broadcasted_iota(jnp.int32, (128, 256), 1).astype(jnp.float32)
            match[gg] = jnp.where(slots == sessions, 1.0, 0.0).T
            for i in range(2):
                win[c, i, gg * 256 : (gg + 1) * 256] = placed(gg, 8 + i).astype(jnp.bfloat16)
        for i in range(2):
            win_copy(i).start()

    def spread_of(gg, t):
        return jnp.dot(exc[gg * 256 : (gg + 1) * 256], wbuf[t], preferred_element_type=jnp.float32)

    def dec_out(t):
        return remote(outbox.at[t], dec_ref.at[t], out_send.at[t], out_recv.at[t], across)

    def tail_out(t):
        return remote(outbox.at[t], tail_ref.at[t], out_send.at[t], out_recv.at[t], across)

    def upsample(t):
        for gg in range(2):
            value = spread_of(gg, t) + placed(gg, t) + convb_ref[...]
            ups[t, gg * 256 : (gg + 1) * 256] = value
            win[c, t + 2, gg * 256 : (gg + 1) * 256] = elu32(value).astype(jnp.bfloat16)
        win_copy(t + 2).start()

    def decode(t):
        win_arrival(t + 2).wait_recv()
        for gg in (1, 0):
            part = slice(gg * 256, (gg + 1) * 256)
            branch = jnp.zeros((256, 256), jnp.float32) + resb_ref[...]
            for k in range(3):
                for h in range(2):
                    branch = branch + jnp.dot(
                        win[h, t + k, part], resbuf[h, k], preferred_element_type=jnp.float32
                    )
            hidden = elu32(branch).astype(jnp.bfloat16)
            value = ups[t, part] + jnp.dot(
                hidden, skipw_ref[...], preferred_element_type=jnp.float32
            ) + skipb_ref[...]
            if gg:
                outbox[t] = value.astype(jnp.bfloat16)
                dec_out(t).start()
            else:
                dec_ref[t] = value.astype(jnp.bfloat16)

    def work(t):
        @pl.when(g == 0)
        def _():
            upsample(t)

            @pl.when(t == 0)
            def _():
                win_arrival(0).wait_recv()
                win_arrival(1).wait_recv()

            @pl.when(t > 0)
            def _():
                decode(t - 1)

        @pl.when(g == 1)
        def _():
            outbox[t] = spread_of(0, t).astype(jnp.bfloat16)
            tail_out(t).start()
            tail_ref[t] = spread_of(1, t).astype(jnp.bfloat16)

    @pl.loop(3, CHUNKS + 3)
    def _(i):
        pump(i)
        settle(i - 3)
        work(i - 3)

    @pl.when(g == 0)
    def _():
        decode(HALF_TAPS - 1)
        for t in range(HALF_TAPS):
            dec_out(t).wait_send()
            tail_out(t).wait_recv()
        for i in range(HALF_TAPS + 2):
            win_copy(i).wait_send()

    @pl.when(g == 1)
    def _():
        for t in range(HALF_TAPS):
            tail_out(t).wait_send()
            dec_out(t).wait_recv()
        cache_copy(0).wait_send()

    for d in range(1, 8):
        lat_copy(d).wait_send()
        cache_copy(d).wait_send()
    res_out.wait_send()
    hop(g, c, 0, partner).wait_send()
    hop(g, c, 1, across).wait_send()
    hop(1 - g, c, 2, partner).wait_send()
    @pl.loop(0, CHUNKS)
    def _(q):
        for s in range(3):

            @pl.when((z < 3) & (z - s >= 0))
            def _():
                up(q, s).wait_send()

            @pl.when((z > 0) & (z + s <= 3))
            def _():
                down(q, s).wait_send()

        for p in range(4):
            side(q, p).wait_send()


def fused(
    latent, conv_weight, conv_bias, tail_cache, input_cache, resume_slot,
    res_weight, res_bias, skip_weight, skip_bias,
):
    taps_first = conv_weight.transpose(1, 0, 2)
    slots = jnp.broadcast_to(resume_slot.astype(jnp.bfloat16)[:, None, None], (8, 16, 256))
    packed = jnp.concatenate(
        [tail_cache, input_cache, jnp.zeros((8, 6, 256), jnp.bfloat16), slots], axis=1
    )
    dma = pltpu.SemaphoreType.DMA
    bf16, f32 = jnp.bfloat16, jnp.float32
    decoded, new_tail = pl.pallas_call(
        fused_kernel,
        out_shape=(
            jax.ShapeDtypeStruct((8, 256, 256), bf16),
            jax.ShapeDtypeStruct((8, 256, 256), bf16),
        ),
        in_specs=[pl.BlockSpec(memory_space=pltpu.VMEM)] * 8,
        out_specs=(pl.BlockSpec(memory_space=pltpu.VMEM),) * 2,
        scratch_shapes=[
            pltpu.VMEM((8, 1024, 256), bf16),
            pltpu.VMEM((2, 2, 256, 512), bf16),
            pltpu.VMEM((16, 32, 256), bf16),
            pltpu.VMEM((512, 1024), bf16),
            pltpu.VMEM((8, 512, 256), f32),
            pltpu.VMEM((2, 10, 512, 256), bf16),
            pltpu.VMEM((2, 3, 256, 256), bf16),
            pltpu.VMEM((8, 256, 256), bf16),
            pltpu.VMEM((2, 256, 128), f32),
            dma((CHUNKS, 10)), dma((CHUNKS, 10)),
            dma((8,)), dma((8,)),
            dma((4,)), dma((4,)),
            dma((8,)), dma((16,)),
            dma((10,)), dma((10,)),
            dma((8,)), dma((8,)),
            dma((4,)),
        ],
        compiler_params=pltpu.CompilerParams(
            collective_id=0, has_side_effects=True, vmem_limit_bytes=48 * 1024 * 1024
        ),
    )(
        latent, taps_first, packed, conv_bias[None, :], res_weight, res_bias[None, :],
        skip_weight, skip_bias[None, :],
    )
    return decoded.transpose(1, 0, 2), new_tail.transpose(1, 0, 2)


def solution(mesh):
    sizes = tuple(mesh.shape[name] for name in ("groups", "streams", "segment"))
    body = fused if sizes == (2, 8, 2) else local
    placed = (
        P(("groups", "streams"), "segment"),
        P("streams", None, "segment"),
        P("segment"),
        P(("groups", "streams"), None, "segment"),
        P(("groups", "streams"), None, "segment"),
        P(("groups", "streams")),
        P(None, "segment", None),
        P(),
        P(None, "segment"),
        P("segment"),
    )
    return jax.shard_map(
        body,
        mesh=mesh,
        in_specs=placed,
        out_specs=(
            P(("groups", "streams"), None, "segment"),
            P(("groups", "streams"), None, "segment"),
        ),
        check_vma=False,
    )
```

```python
import jax
import jax.numpy as jnp
from jax import lax
from jax.experimental import pallas as pl
from jax.experimental.pallas import tpu as pltpu
from jax.sharding import PartitionSpec as P


def apply_elu(values):
    return jnp.where(values > 0, values, jnp.expm1(jnp.minimum(values, 0.0)))


def local(
    latent,
    conv_weight,
    conv_bias,
    tail_cache,
    input_cache,
    resume_slot,
    res_weight,
    res_bias,
    skip_weight,
    skip_bias,
):
    handed = lax.all_to_all(latent, "streams", split_axis=0, concat_axis=0, tiled=True)
    excitation_half = apply_elu(handed.astype(jnp.float32)).astype(jnp.bfloat16)
    excitation = lax.all_gather(excitation_half, "segment", axis=1, tiled=True)
    session_rows = excitation.shape[0]
    tap_count = conv_weight.shape[1]
    half_taps = tap_count // 2
    half_width = conv_weight.shape[2]
    piece = lax.all_gather(conv_weight, "streams", axis=0, tiled=True)
    kernel_rows = piece.reshape(piece.shape[0], tap_count * half_width)
    spread = jnp.dot(excitation, kernel_rows, preferred_element_type=jnp.float32)
    spread = spread.reshape(session_rows, tap_count, half_width)
    fetched_tail, fetched_input, fetched_slot = (
        lax.all_to_all(tail_cache, "streams", split_axis=0, concat_axis=0, tiled=True),
        lax.all_to_all(input_cache, "streams", split_axis=0, concat_axis=0, tiled=True),
        lax.all_to_all(resume_slot, "streams", split_axis=0, concat_axis=0, tiled=True),
    )
    arrivals = fetched_slot.shape[0]
    state_steps = fetched_input.shape[1]
    packed = jnp.concatenate(
        [fetched_tail.reshape(arrivals, -1), fetched_input.reshape(arrivals, -1)], axis=1
    )
    one_hot = (fetched_slot[None, :] == jnp.arange(session_rows, dtype=jnp.int32)[:, None]).astype(
        jnp.bfloat16
    )
    placed = jnp.dot(one_hot, packed, preferred_element_type=jnp.float32)
    prev_tail = placed[:, : half_taps * half_width].reshape(session_rows, half_taps, half_width)
    prev_input = (
        placed[:, half_taps * half_width :]
        .reshape(session_rows, state_steps, half_width)
        .astype(jnp.bfloat16)
    )
    upsampled = spread[:, :half_taps] + prev_tail + conv_bias
    new_tail = spread[:, half_taps:].astype(jnp.bfloat16)
    excited = apply_elu(upsampled).astype(jnp.bfloat16)
    window = jnp.concatenate([prev_input, excited], axis=1)
    hidden_width = res_weight.shape[2]
    partial_value = jnp.zeros((session_rows * half_taps, hidden_width), jnp.float32)
    for offset in range(res_weight.shape[0]):
        frames = window[:, offset : offset + half_taps].reshape(
            session_rows * half_taps, half_width
        )
        partial_value = partial_value + jnp.dot(
            frames, res_weight[offset], preferred_element_type=jnp.float32
        )
    partial_value = partial_value.reshape(session_rows, half_taps, hidden_width)
    summed = lax.psum(partial_value, "segment")
    hidden = apply_elu(summed + res_bias).astype(jnp.bfloat16)
    projected = jnp.dot(
        hidden.reshape(session_rows * half_taps, hidden_width),
        skip_weight,
        preferred_element_type=jnp.float32,
    )
    decoded_block = upsampled + projected.reshape(session_rows, half_taps, half_width) + skip_bias
    return (decoded_block.astype(jnp.bfloat16), new_tail)


CHUNKS = 8
Z_AHEAD = 4
X_AHEAD = 6
HALF_TAPS = 8
MESH = pl.DeviceIdType.MESH


def elu32(values):
    return jnp.where(values > 0, values, jnp.exp(jnp.minimum(values, 0.0)) - 1.0)


def fused_kernel(
    lat_ref, w_ref, cache_ref, convb_ref, resw_ref, resb_ref, skipw_ref, skipb_ref,
    dec_ref, tail_ref,
    wbuf, latb, cach, exc, ups, win, resbuf, outbox, match,
    w_send, w_recv, lat_send, lat_recv, hop_send, hop_recv, c_send, c_recv,
    win_send, win_recv, out_send, out_recv, local_sem,
):
    g = lax.axis_index("groups")
    j = lax.axis_index("streams")
    c = lax.axis_index("segment")
    z, x = j // 2, lax.rem(j, 2)
    per = HALF_TAPS // CHUNKS

    def at(gg, jj, cc):
        return {"groups": gg, "streams": jj, "segment": cc}

    def remote(src, dst, ss, rs, dev):
        return pltpu.make_async_remote_copy(
            src_ref=src, dst_ref=dst, send_sem=ss, recv_sem=rs, device_id=dev, device_id_type=MESH
        )

    partner = at(g, j, 1 - c)
    across = at(1 - g, j, c)

    barrier = pltpu.get_barrier_semaphore()
    for d in range(8):
        peer = lax.rem(j + d, 8)
        if d:
            pl.semaphore_signal(barrier, inc=1, device_id=at(g, peer, c), device_id_type=MESH)
        pl.semaphore_signal(barrier, inc=1, device_id=at(1 - g, peer, c), device_id_type=MESH)
    pl.semaphore_signal(barrier, inc=1, device_id=partner, device_id_type=MESH)

    own_lat = pltpu.make_async_copy(
        lat_ref.at[pl.ds(j * 32, 32)], latb.at[g, c, pl.ds(j * 32, 32)], local_sem.at[0]
    )
    own_w = pltpu.make_async_copy(
        w_ref.at[pl.ds(g * HALF_TAPS, HALF_TAPS)], wbuf.at[:, pl.ds(j * 128, 128)], local_sem.at[1]
    )
    own_res = pltpu.make_async_copy(resw_ref, resbuf.at[c], local_sem.at[2])
    own_cache = pltpu.make_async_copy(cache_ref.at[j], cach.at[j], local_sem.at[3])
    own_w.start()
    own_lat.start()
    own_res.start()

    @pl.when(g == 0)
    def _():
        own_cache.start()

    own_w.wait()
    pl.semaphore_wait(barrier, 16)

    def lat_copy(d):
        peer = lax.rem(j + d, 8)
        return remote(
            lat_ref.at[pl.ds(peer * 32, 32)], latb.at[g, c, pl.ds(j * 32, 32)],
            lat_send.at[d], lat_recv.at[d], at(g, peer, c),
        )

    def lat_arrival(d):
        peer = lax.rem(j + 8 - d, 8)
        return remote(
            lat_ref.at[pl.ds(0, 32)], latb.at[g, c, pl.ds(peer * 32, 32)],
            lat_send.at[d], lat_recv.at[d], at(g, peer, c),
        )

    for d in range(1, 8):
        lat_copy(d).start()

    def w_copy(q, piece, slot, dev):
        block = wbuf.at[pl.ds(q * per, per), pl.ds(piece * 128, 128)]
        return remote(block, block, w_send.at[q, slot], w_recv.at[q, slot], dev)

    def up(q, s):
        return w_copy(q, (z - s) * 2 + x, s, at(g, j + 2, c))

    def up_arrival(q, s):
        return w_copy(q, (z - 1 - s) * 2 + x, s, at(g, j - 2, c))

    def down(q, s):
        return w_copy(q, (z + s) * 2 + x, 3 + s, at(g, j - 2, c))

    def down_arrival(q, s):
        return w_copy(q, (z + 1 + s) * 2 + x, 3 + s, at(g, j + 2, c))

    def side(q, p):
        return w_copy(q, p * 2 + x, 6 + p, at(g, z * 2 + 1 - x, c))

    def side_arrival(q, p):
        return w_copy(q, p * 2 + 1 - x, 6 + p, at(g, z * 2 + 1 - x, c))

    def own_z(q):
        @pl.when(z < 3)
        def _():
            up(q, 0).start()

        @pl.when(z > 0)
        def _():
            down(q, 0).start()

    for q in range(X_AHEAD):
        if q < Z_AHEAD:
            own_z(q)
        side(q, z).start()

    def cache_copy(d):
        peer = lax.rem(j + d, 8)
        return remote(
            cache_ref.at[peer], cach.at[g * 8 + j], c_send.at[d], c_recv.at[g * 8 + d], at(0, peer, c)
        )

    def cache_arrival(gg, d):
        peer = lax.rem(j + 8 - d, 8)
        return remote(
            cache_ref.at[0], cach.at[gg * 8 + peer], c_send.at[d], c_recv.at[gg * 8 + d],
            at(gg, peer, c),
        )

    for d in range(8):
        if d:
            cache_copy(d).start()
        else:

            @pl.when(g == 1)
            def _():
                cache_copy(0).start()

    res_out = remote(resw_ref, resbuf.at[c], hop_send.at[3], hop_recv.at[3], partner)
    res_in = remote(resw_ref, resbuf.at[1 - c], hop_send.at[3], hop_recv.at[3], partner)
    res_out.start()

    def hop(gg, cc, index, dev):
        block = latb.at[gg, cc]
        return remote(block, block, hop_send.at[index], hop_recv.at[index], dev)

    def forward(q, s):
        @pl.when(z - 1 - s >= 0)
        def _():
            up_arrival(q, s).wait_recv()
            if s < 2:

                @pl.when(z < 3)
                def _():
                    up(q, s + 1).start()

            side(q, z - 1 - s).start()

        @pl.when(z + 1 + s <= 3)
        def _():
            down_arrival(q, s).wait_recv()
            if s < 2:

                @pl.when(z > 0)
                def _():
                    down(q, s + 1).start()

            side(q, z + 1 + s).start()

    def pump(i):
        for s in (2, 1, 0):
            q = i - s
            if isinstance(q, int):
                if q >= 0:
                    forward(q, s)
            else:

                @pl.when(q < CHUNKS)
                def _():
                    forward(q, s)

        @pl.when(i + Z_AHEAD < CHUNKS)
        def _():
            own_z(i + Z_AHEAD)

        @pl.when(i + X_AHEAD < CHUNKS)
        def _():
            side(i + X_AHEAD, z).start()

    def settle(q):
        for p in range(4):
            side_arrival(q, p).wait_recv()

    pump(0)
    own_lat.wait()
    for d in range(1, 8):
        lat_arrival(d).wait_recv()
    hop(g, c, 1, across).start()
    hop(g, c, 0, partner).start()
    pump(1)
    hop(1 - g, c, 1, across).wait_recv()
    hop(1 - g, c, 2, partner).start()
    pump(2)
    hop(g, 1 - c, 0, partner).wait_recv()
    hop(1 - g, 1 - c, 2, partner).wait_recv()
    for gg in range(2):
        for h in range(2):
            exc[gg * 256 : (gg + 1) * 256, h * 512 : (h + 1) * 512] = elu32(
                latb[gg, h].astype(jnp.float32)
            ).astype(jnp.bfloat16)

    def win_copy(i):
        return remote(win.at[c, i], win.at[c, i], win_send.at[i], win_recv.at[i], partner)

    def win_arrival(i):
        return remote(win.at[1 - c, i], win.at[1 - c, i], win_send.at[i], win_recv.at[i], partner)

    def placed(gg, row):
        lanes = lax.broadcasted_iota(jnp.int32, (256, 128), 1)
        chosen = jnp.where(lax.rem(lanes, 16) == row, match[gg], 0.0).astype(jnp.bfloat16)
        rows = cach[gg * 8 : (gg + 1) * 8, 0:16].reshape(128, 256)
        return jnp.dot(chosen, rows, preferred_element_type=jnp.float32)

    own_res.wait()
    res_in.wait_recv()

    @pl.when(g == 0)
    def _():
        own_cache.wait()
        for gg in range(2):
            for d in range(8):
                if gg or d:
                    cache_arrival(gg, d).wait_recv()
        for gg in range(2):
            slots = cach[gg * 8 : (gg + 1) * 8, 16:32].reshape(128, 256).astype(jnp.float32)
            sessions = lax.broadcasted_iota(jnp.int32, (128, 256), 1).astype(jnp.float32)
            match[gg] = jnp.where(slots == sessions, 1.0, 0.0).T
            for i in range(2):
                win[c, i, gg * 256 : (gg + 1) * 256] = placed(gg, 8 + i).astype(jnp.bfloat16)
        for i in range(2):
            win_copy(i).start()

    def spread_of(gg, t):
        return jnp.dot(exc[gg * 256 : (gg + 1) * 256], wbuf[t], preferred_element_type=jnp.float32)

    def dec_out(t):
        return remote(outbox.at[t], dec_ref.at[t], out_send.at[t], out_recv.at[t], across)

    def tail_out(t):
        return remote(outbox.at[t], tail_ref.at[t], out_send.at[t], out_recv.at[t], across)

    def upsample(t):
        for gg in range(2):
            value = spread_of(gg, t) + placed(gg, t) + convb_ref[...]
            ups[t, gg * 256 : (gg + 1) * 256] = value
            win[c, t + 2, gg * 256 : (gg + 1) * 256] = elu32(value).astype(jnp.bfloat16)
        win_copy(t + 2).start()

    def decode(t):
        win_arrival(t + 2).wait_recv()
        for gg in (1, 0):
            part = slice(gg * 256, (gg + 1) * 256)
            branch = jnp.zeros((256, 256), jnp.float32) + resb_ref[...]
            for k in range(3):
                for h in range(2):
                    branch = branch + jnp.dot(
                        win[h, t + k, part], resbuf[h, k], preferred_element_type=jnp.float32
                    )
            hidden = elu32(branch).astype(jnp.bfloat16)
            value = ups[t, part] + jnp.dot(
                hidden, skipw_ref[...], preferred_element_type=jnp.float32
            ) + skipb_ref[...]
            if gg:
                outbox[t] = value.astype(jnp.bfloat16)
                dec_out(t).start()
            else:
                dec_ref[t] = value.astype(jnp.bfloat16)

    def work(t):
        @pl.when(g == 0)
        def _():
            upsample(t)

            @pl.when(t == 0)
            def _():
                win_arrival(0).wait_recv()
                win_arrival(1).wait_recv()

            @pl.when(t > 0)
            def _():
                decode(t - 1)

        @pl.when(g == 1)
        def _():
            outbox[t] = spread_of(0, t).astype(jnp.bfloat16)
            tail_out(t).start()
            tail_ref[t] = spread_of(1, t).astype(jnp.bfloat16)

    @pl.loop(3, CHUNKS + 3)
    def _(i):
        pump(i)
        settle(i - 3)
        work(i - 3)

    @pl.when(g == 0)
    def _():
        decode(HALF_TAPS - 1)
        for t in range(HALF_TAPS):
            dec_out(t).wait_send()
            tail_out(t).wait_recv()
        for i in range(HALF_TAPS + 2):
            win_copy(i).wait_send()

    @pl.when(g == 1)
    def _():
        for t in range(HALF_TAPS):
            tail_out(t).wait_send()
            dec_out(t).wait_recv()
        cache_copy(0).wait_send()

    for d in range(1, 8):
        lat_copy(d).wait_send()
        cache_copy(d).wait_send()
    res_out.wait_send()
    hop(g, c, 0, partner).wait_send()
    hop(g, c, 1, across).wait_send()
    hop(1 - g, c, 2, partner).wait_send()
    @pl.loop(0, CHUNKS)
    def _(q):
        for s in range(3):

            @pl.when((z < 3) & (z - s >= 0))
            def _():
                up(q, s).wait_send()

            @pl.when((z > 0) & (z + s <= 3))
            def _():
                down(q, s).wait_send()

        for p in range(4):
            side(q, p).wait_send()


def fused(
    latent, conv_weight, conv_bias, tail_cache, input_cache, resume_slot,
    res_weight, res_bias, skip_weight, skip_bias,
):
    taps_first = conv_weight.transpose(1, 0, 2)
    slots = jnp.broadcast_to(resume_slot.astype(jnp.bfloat16)[:, None, None], (8, 16, 256))
    packed = jnp.concatenate(
        [tail_cache, input_cache, jnp.zeros((8, 6, 256), jnp.bfloat16), slots], axis=1
    )
    dma = pltpu.SemaphoreType.DMA
    bf16, f32 = jnp.bfloat16, jnp.float32
    decoded, new_tail = pl.pallas_call(
        fused_kernel,
        out_shape=(
            jax.ShapeDtypeStruct((8, 256, 256), bf16),
            jax.ShapeDtypeStruct((8, 256, 256), bf16),
        ),
        in_specs=[pl.BlockSpec(memory_space=pltpu.VMEM)] * 8,
        out_specs=(pl.BlockSpec(memory_space=pltpu.VMEM),) * 2,
        scratch_shapes=[
            pltpu.VMEM((8, 1024, 256), bf16),
            pltpu.VMEM((2, 2, 256, 512), bf16),
            pltpu.VMEM((16, 32, 256), bf16),
            pltpu.VMEM((512, 1024), bf16),
            pltpu.VMEM((8, 512, 256), f32),
            pltpu.VMEM((2, 10, 512, 256), bf16),
            pltpu.VMEM((2, 3, 256, 256), bf16),
            pltpu.VMEM((8, 256, 256), bf16),
            pltpu.VMEM((2, 256, 128), f32),
            dma((CHUNKS, 10)), dma((CHUNKS, 10)),
            dma((8,)), dma((8,)),
            dma((4,)), dma((4,)),
            dma((8,)), dma((16,)),
            dma((10,)), dma((10,)),
            dma((8,)), dma((8,)),
            dma((4,)),
        ],
        compiler_params=pltpu.CompilerParams(
            collective_id=0, has_side_effects=True, vmem_limit_bytes=48 * 1024 * 1024
        ),
    )(
        latent, taps_first, packed, conv_bias[None, :], res_weight, res_bias[None, :],
        skip_weight, skip_bias[None, :],
    )
    return decoded.transpose(1, 0, 2), new_tail.transpose(1, 0, 2)


def solution(mesh):
    sizes = tuple(mesh.shape[name] for name in ("groups", "streams", "segment"))
    body = fused if sizes == (2, 8, 2) else local
    placed = (
        P(("groups", "streams"), "segment"),
        P("streams", None, "segment"),
        P("segment"),
        P(("groups", "streams"), None, "segment"),
        P(("groups", "streams"), None, "segment"),
        P(("groups", "streams")),
        P(None, "segment", None),
        P(),
        P(None, "segment"),
        P("segment"),
    )
    return jax.shard_map(
        body,
        mesh=mesh,
        in_specs=placed,
        out_specs=(
            P(("groups", "streams"), None, "segment"),
            P(("groups", "streams"), None, "segment"),
        ),
        check_vma=False,
    )
```
